32 devices in a mesh: role: 2 (over core), row: 4 (over y, x), col: 4 (over z).
Axes of the slice: x: 2, y: 2, z: 4, core: 2. Of those that a mesh axis runs over, the one named last changes fastest.
Arguments:
- queries: bfloat16 [32, 32, 4096], P(('role', 'row', 'col')), may hold values from -6 to 6
- cache_keys: bfloat16 [32, 4096, 512], P(('role', 'row', 'col')), may hold values from -6 to 6
- prompt_value_cache: bfloat16 [32, 4096, 512], P(('role', 'row', 'col')), may hold values from -6 to 6
- new_keys: bfloat16 [32, 32, 512], P(('role', 'row', 'col')), may hold values from -6 to 6
- fresh_token_values: bfloat16 [32, 32, 512], P(('role', 'row', 'col')), may hold values from -6 to 6
- hidden: bfloat16 [32, 32, 2048], P(('role', 'row', 'col')), may hold values from -6 to 6
- out_weight: bfloat16 [4096, 2048], P('row'), may hold values from -0.09375 to 0.09375
- norm_gain: float32 [2048], replicated, may hold values from 0.1 to 1.9
- expert_gate: bfloat16 [32, 2048, 768], P(('role', 'row', 'col')), may hold values from -0.125 to 0.125
- expert_up: bfloat16 [32, 2048, 768], P(('role', 'row', 'col')), may hold values from -0.125 to 0.125
- expert_down: bfloat16 [32, 768, 2048], P(('role', 'row', 'col')), may hold values from -0.21875 to 0.21875
- expert_ids: int32 [32, 32, 8], P(('role', 'row', 'col')), may hold values from 0 to 31, all different within a row; in each aligned block of 32 rows (0 to 31, 32 to 63, ..., all dimensions but the last counted through in order) at most 14 rows name the same one
- routing_gates: float32 [32, 32, 8], P(('role', 'row', 'col')), may hold values from 0.1 to 1
Outputs:
- layer_out: bfloat16 [32, 32, 2048], P(('role', 'row', 'col'))
The draws below stay inside these ranges and needn't reach their ends.
Inputs may be any that keep to these rules, and one draw needn't show every extreme that they name: `expert_ids`: each row names 8 different experts; in the 32 rows of one prompt no expert is named more than 14 times, a bound that some block reaches; every expert is named by some row.
All inputs are finite; a program needn't handle non-finite values.
Results may differ from the reference program's by a relative error of at most 0.014.
Values may be sent and summed in bfloat16 or wider, within the bound.
No kernel may reach another device: no remote copies, remote signals or barrier semaphores. Data moves between devices by JAX's collectives and lax.ppermute only.
A program may use at most 128 MiB of HBM per device.

```python
import math
import jax
import jax.numpy as jnp
import numpy as np
from jax import lax

D = 2048
QUERY_HEADS = 32
KEY_VALUE_HEADS = 4
HEAD_SIZE = 128
FE = 768
TOP = 8
RESPONSE_COUNT = 32
CACHED_TOKENS = 4096
PROMPT_COUNT = 32
EXPERTS = 32
CAP = 14


def starting_queries(key):
    gaussian_component = jax.random.normal(jax.random.fold_in(key, 101), (PROMPT_COUNT, RESPONSE_COUNT, QUERY_HEADS * HEAD_SIZE), jnp.float32)
    return jnp.clip(1.5 * gaussian_component, -6.0, 6.0)


def draw_queries(key, part):
    value_rows = starting_queries(key)
    return value_rows.astype(jnp.bfloat16)


def draw_cache_keys(key, part):
    gaussian_component = jax.random.normal(jax.random.fold_in(key, 103), (PROMPT_COUNT, CACHED_TOKENS, KEY_VALUE_HEADS * HEAD_SIZE), jnp.float32)
    value_rows = jnp.clip(gaussian_component, -6.0, 6.0)
    return value_rows.astype(jnp.bfloat16)


def draw_new_keys(key, part):
    query_foundation = starting_queries(key).reshape(PROMPT_COUNT, RESPONSE_COUNT, KEY_VALUE_HEADS, QUERY_HEADS // KEY_VALUE_HEADS, HEAD_SIZE)
    gaussian_component = jax.random.normal(jax.random.fold_in(key, 104), (PROMPT_COUNT, RESPONSE_COUNT, KEY_VALUE_HEADS, HEAD_SIZE), jnp.float32)
    value_rows = 2.3 * jnp.mean(query_foundation, axis=3) + 0.5 * gaussian_component
    value_rows = jnp.clip(value_rows, -6.0, 6.0)
    return value_rows.reshape(PROMPT_COUNT, RESPONSE_COUNT, KEY_VALUE_HEADS * HEAD_SIZE).astype(jnp.bfloat16)


def block_scale(key, extent, cuts, least, top_value):
    factor_of, own = 1.0, jax.random.fold_in(key, 6)
    for dim, shards_of in cuts:
        steps = jnp.exp(jax.random.uniform(jax.random.fold_in(own, dim), (shards_of,), jnp.float32, least / len(cuts), top_value / len(cuts)))
        factor_of = factor_of * jnp.repeat(steps, extent[dim] // shards_of).reshape([-1 if axis == dim else 1 for axis in range(len(extent))])
    return factor_of


def shared_out(stream_key, own, number, rows, number_of, top, reach, lean):
    ranking = jax.random.permutation(stream_key, number_of)
    packed, common = shares(number_of, rows * top, reach, lean, True), shares(number_of, rows * top, reach, lean, False)
    places = jnp.arange(number_of)

    def named(tallies, rotation):
        used = int((tallies > 0).sum())
        fixed = max(1, used // 4)
        moved = fixed + (places - fixed + rotation * (used - fixed)) % max(1, number_of - fixed)
        return jnp.zeros((number_of,), jnp.int32).at[ranking[jnp.where(places < fixed, places, moved)]].set(jnp.asarray(tallies, jnp.int32))

    tallies = jnp.where(number % 4 == 0, named(packed, number // 4), named(common, number - number // 4 - 1))
    mixed = jax.random.permutation(jax.random.fold_in(own, 3), number_of)
    donor, taker = mixed[0:number_of // 2 * 2:2], mixed[1:number_of // 2 * 2:2]
    slack = jnp.minimum(tallies[donor] - 1, reach - tallies[taker]) // 2
    slack = jnp.where((donor == ranking[0]) | (taker == ranking[0]) | (tallies[taker] == 0), 0, jnp.maximum(slack, 0))
    moved = jax.random.randint(jax.random.fold_in(own, 4), (number_of // 2,), 0, 1 << 20) % (slack + 1)
    tallies = tallies.at[donor].add(-moved).at[taker].add(moved)
    items = jnp.searchsorted(jnp.cumsum(tallies), jnp.arange(rows * top), side="right").astype(jnp.int32)
    table = items.reshape(top, rows).T
    table = table[jax.random.permutation(jax.random.fold_in(own, 1), rows)]
    rotation = jax.random.randint(jax.random.fold_in(own, 2), (rows, 1), 0, top)
    return jnp.take_along_axis(table, (jnp.arange(top)[None, :] + rotation) % top, axis=1)


def shares(amount, total, most, lean, full):
    loads = [(1 << 20) // math.isqrt(grade ** lean) + 1 for grade in range(1, amount + 1)]
    largest = most if full else min(most, max(-(-total // amount), total * loads[0] // sum(loads)))
    least = 1 if total - largest >= amount - 1 else 0
    given, surplus = [largest] + [least] * (amount - 1), total - largest - least * (amount - 1)
    while surplus > 0:
        free = [i for i in range(1, amount) if given[i] < largest] or [i for i in range(1, amount) if given[i] < most]
        whole, left = sum([loads[i] for i in free]), surplus
        for i in free:
            more = min(most - given[i], max(1, left * loads[i] // whole), surplus)
            given[i] = given[i] + more
            surplus = surplus - more
    return np.array(given)


def centred(key, dims, deviation, bound, cuts=(), kind=jnp.bfloat16):
    drawn = jax.random.normal(key, dims, jnp.float32) * deviation
    if len(cuts) > 0:
        drawn = block_scale(key, dims, cuts, -0.22, 0.18) * drawn
    return jnp.clip(drawn, min=-bound, max=bound).astype(kind)


def setup_inputs(seed: int = 0) -> dict:
    arg_keys = jax.random.split(jax.random.key(seed), 14)
    queries = draw_queries(jax.random.fold_in(arg_keys[13], 71), 0)
    cache_keys = draw_cache_keys(jax.random.fold_in(arg_keys[13], 71), 0)
    prompt_value_cache = centred(arg_keys[2], (PROMPT_COUNT, CACHED_TOKENS, KEY_VALUE_HEADS * HEAD_SIZE), 1.0, 6.0, ((0, 32),))
    new_keys = draw_new_keys(jax.random.fold_in(arg_keys[13], 71), 0)
    fresh_token_values = centred(arg_keys[4], (PROMPT_COUNT, RESPONSE_COUNT, KEY_VALUE_HEADS * HEAD_SIZE), 1.0, 6.0, ((0, 32),))
    hidden = centred(arg_keys[5], (PROMPT_COUNT, RESPONSE_COUNT, D), 1.0, 6.0, ((0, 32),))
    out_weight = centred(arg_keys[6], (QUERY_HEADS * HEAD_SIZE, D), (QUERY_HEADS * HEAD_SIZE) ** -0.5, 0.09375, ((0, 4),))
    norm_gain = jnp.clip(1.0 + 0.18 * jax.random.normal(arg_keys[7], (D,), jnp.float32), 0.1, 1.9)
    expert_gate = centred(arg_keys[8], (EXPERTS, D, FE), D ** -0.5, 0.125, ((0, 32),))
    expert_up = centred(arg_keys[9], (EXPERTS, D, FE), D ** -0.5, 0.125, ((0, 32),))
    expert_down = centred(arg_keys[10], (EXPERTS, FE, D), FE ** -0.5, 0.21875, ((0, 32),))
    expert_ids_keys = jax.random.split(jax.random.fold_in(arg_keys[11], 1), PROMPT_COUNT * RESPONSE_COUNT // RESPONSE_COUNT)
    expert_ids_turns = jax.random.permutation(jax.random.fold_in(arg_keys[11], 3), PROMPT_COUNT * RESPONSE_COUNT // RESPONSE_COUNT)
    expert_ids = jax.vmap(lambda own, number: shared_out(jax.random.fold_in(arg_keys[11], 2), own, number, RESPONSE_COUNT, EXPERTS, TOP, CAP, 2))(expert_ids_keys, expert_ids_turns).reshape((PROMPT_COUNT, RESPONSE_COUNT, TOP))
    routing_gates = jnp.clip(jnp.exp(math.log(1.0) - 2.3025851 * jax.random.uniform(arg_keys[12], (PROMPT_COUNT, RESPONSE_COUNT, TOP), jnp.float32) ** block_scale(arg_keys[12], (PROMPT_COUNT, RESPONSE_COUNT, TOP), ((0, 32),), -0.2, 0.2)), 0.1, 1.0)
    return dict(queries=queries, cache_keys=cache_keys, prompt_value_cache=prompt_value_cache, new_keys=new_keys, fresh_token_values=fresh_token_values, hidden=hidden, out_weight=out_weight, norm_gain=norm_gain, expert_gate=expert_gate, expert_up=expert_up, expert_down=expert_down, expert_ids=expert_ids, routing_gates=routing_gates)


def attend_prompt(operands):
    query_rows, keys_cache, values_cache, keys_new, values_new = operands
    heads_per_group = QUERY_HEADS // KEY_VALUE_HEADS
    score_scale = HEAD_SIZE ** (-0.5)
    pieces = []
    for key_value_head in range(KEY_VALUE_HEADS):
        first_col = key_value_head * heads_per_group * HEAD_SIZE
        q_block = query_rows[:, first_col:first_col + heads_per_group * HEAD_SIZE].reshape(RESPONSE_COUNT * heads_per_group, HEAD_SIZE)
        k_block = keys_cache[:, key_value_head * HEAD_SIZE:(key_value_head + 1) * HEAD_SIZE]
        v_block = values_cache[:, key_value_head * HEAD_SIZE:(key_value_head + 1) * HEAD_SIZE]
        own_key = jnp.repeat(keys_new[:, key_value_head * HEAD_SIZE:(key_value_head + 1) * HEAD_SIZE], heads_per_group, axis=0)
        own_value = jnp.repeat(values_new[:, key_value_head * HEAD_SIZE:(key_value_head + 1) * HEAD_SIZE], heads_per_group, axis=0)
        scores = jnp.dot(q_block, k_block.T, preferred_element_type=jnp.float32) * score_scale
        own_score = lax.optimization_barrier(jnp.sum(q_block.astype(jnp.float32) * own_key.astype(jnp.float32), axis=1)) * score_scale
        highest = jnp.maximum(lax.optimization_barrier(jnp.max(scores, axis=1)), own_score)
        exp_scores = jnp.exp(scores - highest[:, None])
        own_exp = jnp.exp(own_score - highest)
        denominator = lax.optimization_barrier(jnp.sum(exp_scores, axis=1)) + own_exp
        weights = (exp_scores / denominator[:, None]).astype(jnp.bfloat16)
        own_weight = (own_exp / denominator).astype(jnp.bfloat16)
        mixed_rows = jnp.dot(weights, v_block, preferred_element_type=jnp.float32)
        mixed_rows = mixed_rows + own_weight.astype(jnp.float32)[:, None] * own_value.astype(jnp.float32)
        pieces.append(mixed_rows.astype(jnp.bfloat16).reshape(RESPONSE_COUNT, heads_per_group * HEAD_SIZE))
    return jnp.concatenate(pieces, axis=1)

def reference(queries, cache_keys, prompt_value_cache, new_keys, fresh_token_values, hidden, out_weight, norm_gain, expert_gate, expert_up, expert_down, expert_ids, routing_gates):
    attended = lax.map(attend_prompt, (queries, cache_keys, prompt_value_cache, new_keys, fresh_token_values))
    projected = jnp.dot(attended.reshape(PROMPT_COUNT * RESPONSE_COUNT, QUERY_HEADS * HEAD_SIZE), out_weight, preferred_element_type=jnp.float32)
    mid_rows = hidden.reshape(PROMPT_COUNT * RESPONSE_COUNT, D).astype(jnp.float32) + projected
    mean_square = lax.optimization_barrier(jnp.mean(mid_rows * mid_rows, axis=1, keepdims=True))
    normed = (mid_rows * lax.rsqrt(mean_square + 1e-06) * norm_gain[None, :]).astype(jnp.bfloat16)
    normed_three = normed.reshape(PROMPT_COUNT, RESPONSE_COUNT, D)
    flat_ids = expert_ids.reshape(PROMPT_COUNT, RESPONSE_COUNT * TOP).astype(jnp.int32)
    onehot = (flat_ids[:, :, None] == jnp.arange(EXPERTS, dtype=jnp.int32)[None, None, :]).astype(jnp.int32)
    rank_before = jnp.cumsum(onehot, axis=1) - onehot
    slot_index = lax.optimization_barrier(jnp.sum(rank_before * onehot, axis=2)).astype(jnp.int32)
    position = (flat_ids * CAP + slot_index).astype(jnp.int32)
    pair_rows = jnp.broadcast_to((jnp.arange(RESPONSE_COUNT * TOP, dtype=jnp.int32) // TOP)[None, :], (PROMPT_COUNT, RESPONSE_COUNT * TOP))
    prompt_ids = jnp.broadcast_to(jnp.arange(PROMPT_COUNT, dtype=jnp.int32)[:, None], (PROMPT_COUNT, RESPONSE_COUNT * TOP))
    sources = jnp.full((PROMPT_COUNT, EXPERTS * CAP), -1, jnp.int32).at[prompt_ids, position].set(pair_rows)

    def serve_expert(operands):
        expert_num, gate_matrix, up_matrix, down_matrix = operands
        table_rows = lax.dynamic_slice_in_dim(sources, (expert_num * CAP).astype(jnp.int32), CAP, 1)
        safe_rows = jnp.maximum(table_rows, 0).astype(jnp.int32)
        block = jnp.take_along_axis(normed_three, safe_rows[:, :, None], axis=1)
        block = jnp.where((table_rows >= 0)[:, :, None], block, jnp.zeros_like(block))
        flat_block = block.reshape(PROMPT_COUNT * CAP, D)
        gate_part = jnp.dot(flat_block, gate_matrix, preferred_element_type=jnp.float32)
        up_part = jnp.dot(flat_block, up_matrix, preferred_element_type=jnp.float32)
        act = (jax.nn.silu(gate_part) * up_part).astype(jnp.bfloat16)
        returned = jnp.dot(act, down_matrix, preferred_element_type=jnp.float32).astype(jnp.bfloat16)
        return returned.reshape(PROMPT_COUNT, CAP, D)
    served = lax.map(serve_expert, (jnp.arange(EXPERTS, dtype=jnp.int32), expert_gate, expert_up, expert_down))
    picked = served[flat_ids, prompt_ids, slot_index]
    picked = picked.reshape(PROMPT_COUNT, RESPONSE_COUNT, TOP, D).astype(jnp.float32)
    expert_sum = lax.optimization_barrier(jnp.sum(picked * routing_gates[:, :, :, None], axis=2))
    return (mid_rows.reshape(PROMPT_COUNT, RESPONSE_COUNT, D) + expert_sum).astype(jnp.bfloat16)
```

```python
import functools

import jax
import jax.numpy as jnp
from jax import lax
from jax.experimental import pallas as pl
from jax.experimental.pallas import tpu as pltpu
from jax.sharding import PartitionSpec as P


HEAD_SIZE = 128
LOG2E = 1.4426950408889634
F32 = jnp.float32
BF16 = jnp.bfloat16
LANES = 128


def attention_kernel(
    order_ref, q_ref, k_ref, v_ref, nk_ref, nv_ref, *rest, heads, groups, sub
):
    outs, (m_s, l_s, acc_s) = rest[:heads], rest[heads:]
    step, part = pl.program_id(0), pl.program_id(1)
    scale = HEAD_SIZE ** (-0.5) * LOG2E
    q_rows = q_ref[0]
    q = jnp.concatenate(
        [q_rows[:, h * HEAD_SIZE : (h + 1) * HEAD_SIZE] for h in range(groups)], axis=0
    )

    @pl.when(part == 0)
    def _():
        own_key = jnp.concatenate([nk_ref[0]] * groups, axis=0).astype(F32)
        own_value = jnp.concatenate([nv_ref[0]] * groups, axis=0).astype(F32)
        own = jnp.sum(q.astype(F32) * own_key, axis=1, keepdims=True) * scale
        m_s[...] = jnp.broadcast_to(own, m_s.shape)
        l_s[...] = jnp.full(l_s.shape, 1.0 / LANES, F32)
        acc_s[...] = own_value

    def scores(j):
        keys = k_ref[0, j * sub : (j + 1) * sub, :]
        return (
            lax.dot_general(q, keys, (((1,), (1,)), ((), ())), preferred_element_type=F32)
            * scale
        )

    top, total, acc = m_s[:, :1], l_s[...], acc_s[...]
    steps = k_ref.shape[1] // sub
    current = scores(0)
    for j in range(steps):
        following = scores(j + 1) if j + 1 < steps else None
        new_top = jnp.maximum(top, jnp.max(current, axis=1, keepdims=True))
        fade = jnp.exp2(top - new_top)
        p = jnp.exp2(current - new_top)
        lane_sum = p[:, :LANES]
        for c in range(1, sub // LANES):
            lane_sum = lane_sum + p[:, c * LANES : (c + 1) * LANES]
        total = total * fade + lane_sum
        acc = acc * fade + jnp.dot(
            p.astype(BF16), v_ref[0, j * sub : (j + 1) * sub, :], preferred_element_type=F32
        )
        top, current = new_top, following
    m_s[...] = jnp.broadcast_to(top, m_s.shape)
    l_s[...] = total
    acc_s[...] = acc

    @pl.when(part == pl.num_programs(1) - 1)
    def _():
        result = (acc / jnp.sum(total, axis=1, keepdims=True)).astype(BF16)
        rows = q_rows.shape[0]
        wide = jnp.concatenate(
            [result[h * rows : (h + 1) * rows] for h in range(groups)], axis=1
        )
        for i in range(heads):

            @pl.when(step == i)
            def _(i=i):
                outs[i][...] = wide


def attend(order, queries, keys, values, new_keys, new_values):
    heads = order.shape[0]
    rows = queries.shape[1]
    kv_heads = keys.shape[2] // HEAD_SIZE
    width = queries.shape[2] // kv_heads
    groups = width // HEAD_SIZE
    tokens = keys.shape[1]
    part = min(tokens, 2048)
    sub = min(part, 512)
    per_row = groups * rows
    wide = pl.BlockSpec((1, rows, width), lambda i, j, o: (0, 0, o[i]))
    cache = pl.BlockSpec((1, part, HEAD_SIZE), lambda i, j, o: (0, j, o[i]))
    fresh = pl.BlockSpec((1, rows, HEAD_SIZE), lambda i, j, o: (0, 0, o[i]))
    return pl.pallas_call(
        functools.partial(attention_kernel, heads=heads, groups=groups, sub=sub),
        grid_spec=pltpu.PrefetchScalarGridSpec(
            num_scalar_prefetch=1,
            grid=(heads, tokens // part),
            in_specs=[wide, cache, cache, fresh, fresh],
            out_specs=[pl.BlockSpec((rows, width), lambda i, j, o: (0, 0))] * heads,
            scratch_shapes=[
                pltpu.VMEM((per_row, LANES), F32),
                pltpu.VMEM((per_row, LANES), F32),
                pltpu.VMEM((per_row, HEAD_SIZE), F32),
            ],
        ),
        out_shape=[jax.ShapeDtypeStruct((rows, width), BF16)] * heads,
        compiler_params=pltpu.CompilerParams(
            dimension_semantics=("arbitrary", "arbitrary")
        ),
        cost_estimate=pl.CostEstimate(
            flops=4 * heads * per_row * tokens * HEAD_SIZE,
            transcendentals=heads * per_row * tokens,
            bytes_accessed=4 * heads * tokens * HEAD_SIZE,
        ),
    )(order, queries, keys, values, new_keys, new_values)


def project_kernel(*refs, count):
    x_refs, w_ref, outs = refs[:count], refs[count], refs[count + 1 :]
    rows = x_refs[0].shape[0]
    x = jnp.concatenate([r[...] for r in x_refs], axis=0) if count > 1 else x_refs[0][...]
    y = jnp.dot(x, w_ref[...], preferred_element_type=F32)
    for i in range(count):
        outs[i][...] = y[i * rows : (i + 1) * rows].astype(outs[i].dtype)


def project(blocks, weight, dtype):
    count = len(blocks)
    rows, depth = blocks[0].shape
    width = weight.shape[1]
    tile = min(width, 512)
    return pl.pallas_call(
        functools.partial(project_kernel, count=count),
        grid=(width // tile,),
        in_specs=[pl.BlockSpec((rows, depth), lambda n: (0, 0))] * count
        + [pl.BlockSpec((depth, tile), lambda n: (0, n))],
        out_specs=[pl.BlockSpec((rows, tile), lambda n: (0, n))] * count,
        out_shape=[jax.ShapeDtypeStruct((rows, width), dtype)] * count,
        compiler_params=pltpu.CompilerParams(dimension_semantics=("arbitrary",)),
        cost_estimate=pl.CostEstimate(
            flops=2 * count * rows * depth * width,
            transcendentals=0,
            bytes_accessed=2 * depth * width,
        ),
    )(*blocks, weight)


def norm_kernel(*refs, count):
    own_ref, parts = refs[0], refs[1 : 1 + count]
    hidden_ref, gain_ref, meta_ref, mid_ref, token_ref = refs[1 + count :]
    total = own_ref[...]
    for r in parts:
        total = total + r[...].astype(F32)
    mid = hidden_ref[0].astype(F32) + total
    width = mid.shape[1]
    mean_square = jnp.mean(mid * mid, axis=1, keepdims=True)
    mid_ref[...] = mid
    token_ref[:, :width] = (mid * lax.rsqrt(mean_square + 1e-06) * gain_ref[...]).astype(BF16)
    token_ref[:, width:] = meta_ref[...]


def norm_rows(own, parts, hidden, gain, meta):
    rows, width = own.shape
    return pl.pallas_call(
        functools.partial(norm_kernel, count=len(parts)),
        out_shape=[
            jax.ShapeDtypeStruct((rows, width), F32),
            jax.ShapeDtypeStruct((rows, width + meta.shape[1]), BF16),
        ],
        cost_estimate=pl.CostEstimate(
            flops=8 * rows * width, transcendentals=0, bytes_accessed=16 * rows * width
        ),
    )(own, *parts, hidden, gain[None, :], meta)


def expert_kernel(*refs, near, far, top):
    count = near + far
    expert_ref, blocks = refs[0], refs[1 : 1 + count]
    wg_ref, wu_ref, wd_ref = refs[1 + count : 4 + count]
    outs, (x_s, coef_s, acc_s) = refs[4 + count : 4 + 2 * count], refs[4 + 2 * count :]
    step, steps = pl.program_id(0), pl.num_programs(0)
    rows = blocks[0].shape[0]
    width = x_s.shape[1]

    @pl.when(step == 0)
    def _():
        expert = expert_ref[0].astype(F32)
        for i in range(count):
            x_s[i * rows : (i + 1) * rows, :] = blocks[i][:, :width]
            meta = blocks[i][:, width:].astype(F32)
            ids = meta[:, :top]
            gates = meta[:, top : 2 * top] + meta[:, 2 * top : 3 * top]
            coef = jnp.sum(jnp.where(ids == expert, gates, 0.0), axis=1, keepdims=True)
            coef_s[i * rows : (i + 1) * rows, :] = jnp.broadcast_to(coef, (rows, LANES))

    x = x_s[...]
    gate = jnp.dot(x, wg_ref[0], preferred_element_type=F32)
    up = jnp.dot(x, wu_ref[0], preferred_element_type=F32)
    act = (gate / (1.0 + jnp.exp(-gate)) * up).astype(BF16)
    down = jnp.dot(act, wd_ref[0], preferred_element_type=F32)

    @pl.when(step == 0)
    def _():
        acc_s[...] = down

    @pl.when(jnp.logical_and(step > 0, step < steps - 1))
    def _():
        acc_s[...] += down

    @pl.when(step == steps - 1)
    def _():
        total = (acc_s[...] + down) * coef_s[:, :1]
        for i in range(count):
            outs[i][...] = total[i * rows : (i + 1) * rows].astype(BF16)


def run_expert(expert, near, far, wg, wu, wd, top):
    count = len(near) + len(far)
    rows, wide = near[0].shape
    width, hidden = wg.shape[1:]
    tile = min(hidden, 256)
    outs = pl.pallas_call(
        functools.partial(expert_kernel, near=len(near), far=len(far), top=top),
        grid_spec=pltpu.PrefetchScalarGridSpec(
            num_scalar_prefetch=1,
            grid=(hidden // tile,),
            in_specs=[pl.BlockSpec((rows, wide), lambda f, e: (0, 0))] * count
            + [
                pl.BlockSpec((1, width, tile), lambda f, e: (0, 0, f)),
                pl.BlockSpec((1, width, tile), lambda f, e: (0, 0, f)),
                pl.BlockSpec((1, tile, width), lambda f, e: (0, f, 0)),
            ],
            out_specs=[pl.BlockSpec((rows, width), lambda f, e: (0, 0))] * count,
            scratch_shapes=[
                pltpu.VMEM((count * rows, width), BF16),
                pltpu.VMEM((count * rows, LANES), F32),
                pltpu.VMEM((count * rows, width), F32),
            ],
        ),
        out_shape=[jax.ShapeDtypeStruct((rows, width), BF16)] * count,
        compiler_params=pltpu.CompilerParams(dimension_semantics=("arbitrary",)),
        cost_estimate=pl.CostEstimate(
            flops=6 * count * rows * width * hidden,
            transcendentals=count * rows * hidden,
            bytes_accessed=6 * width * hidden,
        ),
    )(expert, *near, *far, wg, wu, wd)
    return outs[: len(near)], outs[len(near) :]


def add(*terms):
    total = terms[0].astype(F32)
    for t in terms[1:]:
        total = total + t.astype(F32)
    return total


def per_device(
    queries,
    cache_keys,
    prompt_value_cache,
    new_keys,
    fresh_token_values,
    hidden,
    out_weight,
    norm_gain,
    expert_gate,
    expert_up,
    expert_down,
    expert_ids,
    routing_gates,
):
    roles, row_count, col_count = (lax.axis_size(a) for a in ("role", "row", "col"))
    plane = row_count * col_count
    experts = roles * plane
    row = lax.axis_index("row")
    expert = lax.axis_index(("role", "row", "col"))
    top = expert_ids.shape[2]

    def by_row(x, mask):
        return lax.ppermute(x, "row", [(i, i ^ mask) for i in range(row_count)])

    def by_plane(x, mask):
        return lax.ppermute(x, ("row", "col"), [(i, i ^ mask) for i in range(plane)])

    def by_role(x):
        return lax.ppermute(x, "role", [(i, i ^ 1) for i in range(roles)])

    order = jnp.bitwise_xor(row, jnp.arange(1, row_count, dtype=jnp.int32)).astype(jnp.int32)
    caches = (queries, cache_keys, prompt_value_cache, new_keys, fresh_token_values)
    foreign = attend(order, *caches)
    arrived = [by_row(foreign[m - 1], m) for m in range(1, row_count)]
    own = attend(row.astype(jnp.int32)[None], *caches)[0]
    products = project(arrived, out_weight, BF16)
    parts = [by_row(products[m - 1], m) for m in range(1, row_count)]
    own_product = project([own], out_weight, F32)[0]

    gates = routing_gates[0]
    gates_high = lax.reduce_precision(gates, 8, 7)
    meta = jnp.concatenate([expert_ids[0].astype(F32), gates_high, gates - gates_high], axis=1)
    meta = jnp.pad(meta, ((0, 0), (0, -meta.shape[1] % LANES))).astype(BF16)
    mid_rows, token = norm_rows(own_product, parts, hidden, norm_gain, meta)

    half = col_count // 2
    members = [r * col_count + c for r in range(row_count) for c in range(half)]
    two_stage = row_count == 4 and half == 2
    mx, my, mz = col_count, 2 * col_count, 1

    def gather(x):
        if not two_stage:
            return {m: (by_plane(x, m) if m else x) for m in members}
        body = by_plane(x, mx ^ my ^ mz)
        bx, by, bz = by_plane(x, mx), by_plane(x, my), by_plane(x, mz)
        return {
            0: x,
            mx: bx,
            my: by,
            mz: bz,
            mx ^ my: by_plane(by, mx),
            my ^ mz: by_plane(bz, my),
            mz ^ mx: by_plane(bx, mz),
            mx ^ my ^ mz: body,
        }

    def scatter(y):
        if not two_stage:
            return add(*[by_plane(y[m], m) if m else y[m] for m in members])
        body = by_plane(y[mx ^ my ^ mz], mx ^ my ^ mz)
        via_x, via_y, via_z = by_plane(y[mx ^ my], mx), by_plane(y[my ^ mz], my), by_plane(y[mz ^ mx], mz)
        to_y = by_plane(add(y[my], via_x).astype(BF16), my)
        to_z = by_plane(add(y[mz], via_y).astype(BF16), mz)
        to_x = by_plane(add(y[mx], via_z).astype(BF16), mx)
        return add(y[0], body, to_x, to_y, to_z)

    mirrored = by_plane(token, half)
    expert_number = expert.astype(jnp.int32)[None]
    results = []
    for source in (token, mirrored):
        near = gather(source)
        far = {m: by_role(near[m]) for m in members}
        partial = {}
        for first in range(0, len(members), 8):
            chunk = members[first : first + 8]
            own_out, far_out = run_expert(
                expert_number,
                [near[m] for m in chunk],
                [far[m] for m in chunk],
                expert_gate,
                expert_up,
                expert_down,
                top,
            )
            for m, a, b in zip(chunk, own_out, far_out):
                partial[m] = add(a, by_role(b)).astype(BF16)
        results.append(scatter(partial))
    returned = by_plane(results[1].astype(BF16), half)
    return (mid_rows + results[0] + returned.astype(F32)).astype(BF16)[None]


def solution(mesh):
    split = P(("role", "row", "col"), None, None)
    return jax.shard_map(
        per_device,
        mesh=mesh,
        in_specs=(split,) * 6 + (P("row", None), P()) + (split,) * 5,
        out_specs=split,
        check_vma=False,
    )
```

```python
import functools

import jax
import jax.numpy as jnp
from jax import lax
from jax.experimental import pallas as pl
from jax.experimental.pallas import tpu as pltpu
from jax.sharding import PartitionSpec as P


HEAD_SIZE = 128
LOG2E = 1.4426950408889634
F32 = jnp.float32
BF16 = jnp.bfloat16
LANES = 128


def attention_kernel(
    order_ref, q_ref, k_ref, v_ref, nk_ref, nv_ref, *rest, heads, groups, sub
):
    outs, (m_s, l_s, acc_s) = rest[:heads], rest[heads:]
    step, part = pl.program_id(0), pl.program_id(1)
    scale = HEAD_SIZE ** (-0.5) * LOG2E
    q_rows = q_ref[0]
    q = jnp.concatenate(
        [q_rows[:, h * HEAD_SIZE : (h + 1) * HEAD_SIZE] for h in range(groups)], axis=0
    )

    @pl.when(part == 0)
    def _():
        own_key = jnp.concatenate([nk_ref[0]] * groups, axis=0).astype(F32)
        own_value = jnp.concatenate([nv_ref[0]] * groups, axis=0).astype(F32)
        own = jnp.sum(q.astype(F32) * own_key, axis=1, keepdims=True) * scale
        m_s[...] = jnp.broadcast_to(own, m_s.shape)
        l_s[...] = jnp.full(l_s.shape, 1.0 / LANES, F32)
        acc_s[...] = own_value

    def scores(j):
        keys = k_ref[0, j * sub : (j + 1) * sub, :]
        return (
            lax.dot_general(q, keys, (((1,), (1,)), ((), ())), preferred_element_type=F32)
            * scale
        )

    top, total, acc = m_s[:, :1], l_s[...], acc_s[...]
    steps = k_ref.shape[1] // sub
    current = scores(0)
    for j in range(steps):
        following = scores(j + 1) if j + 1 < steps else None
        new_top = jnp.maximum(top, jnp.max(current, axis=1, keepdims=True))
        fade = jnp.exp2(top - new_top)
        p = jnp.exp2(current - new_top)
        lane_sum = p[:, :LANES]
        for c in range(1, sub // LANES):
            lane_sum = lane_sum + p[:, c * LANES : (c + 1) * LANES]
        total = total * fade + lane_sum
        acc = acc * fade + jnp.dot(
            p.astype(BF16), v_ref[0, j * sub : (j + 1) * sub, :], preferred_element_type=F32
        )
        top, current = new_top, following
    m_s[...] = jnp.broadcast_to(top, m_s.shape)
    l_s[...] = total
    acc_s[...] = acc

    @pl.when(part == pl.num_programs(1) - 1)
    def _():
        result = (acc / jnp.sum(total, axis=1, keepdims=True)).astype(BF16)
        rows = q_rows.shape[0]
        wide = jnp.concatenate(
            [result[h * rows : (h + 1) * rows] for h in range(groups)], axis=1
        )
        for i in range(heads):

            @pl.when(step == i)
            def _(i=i):
                outs[i][...] = wide


def attend(order, queries, keys, values, new_keys, new_values):
    heads = order.shape[0]
    rows = queries.shape[1]
    kv_heads = keys.shape[2] // HEAD_SIZE
    width = queries.shape[2] // kv_heads
    groups = width // HEAD_SIZE
    tokens = keys.shape[1]
    part = min(tokens, 4096)
    sub = min(part, 2048)
    per_row = groups * rows
    wide = pl.BlockSpec((1, rows, width), lambda i, j, o: (0, 0, o[i]))
    cache = pl.BlockSpec((1, part, HEAD_SIZE), lambda i, j, o: (0, j, o[i]))
    fresh = pl.BlockSpec((1, rows, HEAD_SIZE), lambda i, j, o: (0, 0, o[i]))
    return pl.pallas_call(
        functools.partial(attention_kernel, heads=heads, groups=groups, sub=sub),
        grid_spec=pltpu.PrefetchScalarGridSpec(
            num_scalar_prefetch=1,
            grid=(heads, tokens // part),
            in_specs=[wide, cache, cache, fresh, fresh],
            out_specs=[pl.BlockSpec((rows, width), lambda i, j, o: (0, 0))] * heads,
            scratch_shapes=[
                pltpu.VMEM((per_row, LANES), F32),
                pltpu.VMEM((per_row, LANES), F32),
                pltpu.VMEM((per_row, HEAD_SIZE), F32),
            ],
        ),
        out_shape=[jax.ShapeDtypeStruct((rows, width), BF16)] * heads,
        compiler_params=pltpu.CompilerParams(
            dimension_semantics=("arbitrary", "arbitrary")
        ),
        cost_estimate=pl.CostEstimate(
            flops=4 * heads * per_row * tokens * HEAD_SIZE,
            transcendentals=heads * per_row * tokens,
            bytes_accessed=4 * heads * tokens * HEAD_SIZE,
        ),
    )(order, queries, keys, values, new_keys, new_values)


def project_kernel(*refs, count):
    x_refs, w_ref, outs = refs[:count], refs[count], refs[count + 1 :]
    rows = x_refs[0].shape[0]
    x = jnp.concatenate([r[...] for r in x_refs], axis=0) if count > 1 else x_refs[0][...]
    y = jnp.dot(x, w_ref[...], preferred_element_type=F32)
    for i in range(count):
        outs[i][...] = y[i * rows : (i + 1) * rows].astype(outs[i].dtype)


def project(blocks, weight, dtype):
    count = len(blocks)
    rows, depth = blocks[0].shape
    width = weight.shape[1]
    tile = min(width, 1024)
    kinds = [dtype] * (count - 1) + [F32]
    return pl.pallas_call(
        functools.partial(project_kernel, count=count),
        grid=(width // tile,),
        in_specs=[pl.BlockSpec((rows, depth), lambda n: (0, 0))] * count
        + [pl.BlockSpec((depth, tile), lambda n: (0, n))],
        out_specs=[pl.BlockSpec((rows, tile), lambda n: (0, n))] * count,
        out_shape=[jax.ShapeDtypeStruct((rows, width), kind) for kind in kinds],
        compiler_params=pltpu.CompilerParams(dimension_semantics=("arbitrary",)),
        cost_estimate=pl.CostEstimate(
            flops=2 * count * rows * depth * width,
            transcendentals=0,
            bytes_accessed=2 * depth * width,
        ),
    )(*blocks, weight)


def norm_kernel(*refs, count):
    own_ref, parts = refs[0], refs[1 : 1 + count]
    hidden_ref, gain_ref, meta_ref, mid_ref, token_ref = refs[1 + count :]
    total = own_ref[...]
    for r in parts:
        total = total + r[...].astype(F32)
    mid = hidden_ref[0].astype(F32) + total
    width = mid.shape[1]
    mean_square = jnp.mean(mid * mid, axis=1, keepdims=True)
    mid_ref[...] = mid
    token_ref[:, :width] = (mid * lax.rsqrt(mean_square + 1e-06) * gain_ref[...]).astype(BF16)
    token_ref[:, width:] = meta_ref[...]


def norm_rows(own, parts, hidden, gain, meta):
    rows, width = own.shape
    return pl.pallas_call(
        functools.partial(norm_kernel, count=len(parts)),
        out_shape=[
            jax.ShapeDtypeStruct((rows, width), F32),
            jax.ShapeDtypeStruct((rows, width + meta.shape[1]), BF16),
        ],
        cost_estimate=pl.CostEstimate(
            flops=8 * rows * width, transcendentals=0, bytes_accessed=16 * rows * width
        ),
    )(own, *parts, hidden, gain[None, :], meta)


def expert_kernel(numbers_ref, *refs, count, roles, top, cuts):
    blocks, refs = refs[:count], refs[count:]
    gate_hbm, up_hbm, down_hbm = (refs[i * roles : (i + 1) * roles] for i in range(3))
    outs, (x_s, act_s, gate_s, up_s, down_s, sems) = refs[3 * roles : -6], refs[-6:]
    rows = blocks[0].shape[0]
    width, hidden = gate_hbm[0].shape[1:]

    def fetch(e, first, last):
        cut = pl.ds(first, last - first)
        return [
            pltpu.make_async_copy(gate_hbm[e].at[0, :, cut], gate_s.at[e, :, cut], sems.at[0, e, cuts.index(first)]),
            pltpu.make_async_copy(up_hbm[e].at[0, :, cut], up_s.at[e, :, cut], sems.at[1, e, cuts.index(first)]),
        ]

    def fetch_down(e):
        return [pltpu.make_async_copy(down_hbm[e].at[0], down_s.at[pl.ds(e * hidden, hidden), :], sems.at[2, e, 0])]

    spans = [(e, i, j) for e in range(roles) for i, j in zip(cuts[:-1], cuts[1:])]
    queue = [fetch(*span) for span in spans]
    downs = [fetch_down(e) for e in range(roles)]
    for copy in queue[0]:
        copy.start()

    coefs = [[] for _ in range(roles)]
    for i in range(count):
        x_s[i * rows : (i + 1) * rows, :] = blocks[i][:, :width]
        meta = blocks[i][:, width:].astype(F32)
        ids = meta[:, :top]
        gates = meta[:, top : 2 * top] + meta[:, 2 * top : 3 * top]
        for e in range(roles):
            mine = ids == numbers_ref[e].astype(F32)
            coefs[e].append(jnp.sum(jnp.where(mine, gates, 0.0), axis=1, keepdims=True))
    coefs = [jnp.concatenate(c, axis=0) for c in coefs]

    for n, (e, first, last) in enumerate(spans):
        for copy in queue[n]:
            copy.wait()
        if n == 0:
            for later in queue[1:] + downs:
                for copy in later:
                    copy.start()
        x = x_s[...]
        gate = jnp.dot(x, gate_s[e, :, first:last], preferred_element_type=F32)
        up = jnp.dot(x, up_s[e, :, first:last], preferred_element_type=F32)
        act = gate / (1.0 + jnp.exp(-gate)) * up * coefs[e]
        act_s[:, e * hidden + first : e * hidden + last] = act.astype(BF16)
    for copy in sum(downs, []):
        copy.wait()
    total = jnp.dot(act_s[...], down_s[...], preferred_element_type=F32)
    for i in range(count):
        outs[i][...] = total[i * rows : (i + 1) * rows].astype(BF16)


def run_experts(numbers, blocks, gates, ups, downs, top):
    count, roles = len(blocks), len(gates)
    rows, wide = blocks[0].shape
    width, hidden = gates[0].shape[1:]
    cuts = (0, hidden // 3, hidden) if hidden % 384 == 0 else (0, hidden)
    whole = pl.BlockSpec(memory_space=pltpu.VMEM)
    return pl.pallas_call(
        functools.partial(expert_kernel, count=count, roles=roles, top=top, cuts=cuts),
        in_specs=[pl.BlockSpec(memory_space=pltpu.SMEM)]
        + [whole] * count
        + [pl.BlockSpec(memory_space=pl.ANY)] * (3 * roles),
        out_specs=[whole] * count,
        out_shape=[jax.ShapeDtypeStruct((rows, width), BF16)] * count,
        scratch_shapes=[
            pltpu.VMEM((count * rows, width), BF16),
            pltpu.VMEM((count * rows, roles * hidden), BF16),
            pltpu.VMEM((roles, width, hidden), BF16),
            pltpu.VMEM((roles, width, hidden), BF16),
            pltpu.VMEM((roles * hidden, width), BF16),
            pltpu.SemaphoreType.DMA((3, roles, len(cuts))),
        ],
        cost_estimate=pl.CostEstimate(
            flops=6 * roles * count * rows * width * hidden,
            transcendentals=roles * count * rows * hidden,
            bytes_accessed=6 * roles * width * hidden,
        ),
    )(numbers, *blocks, *gates, *ups, *downs)


def add(*terms):
    total = terms[0].astype(F32)
    for t in terms[1:]:
        total = total + t.astype(F32)
    return total


def per_device(
    queries,
    cache_keys,
    prompt_value_cache,
    new_keys,
    fresh_token_values,
    hidden,
    out_weight,
    norm_gain,
    expert_gate,
    expert_up,
    expert_down,
    expert_ids,
    routing_gates,
):
    roles, row_count, col_count = (lax.axis_size(a) for a in ("role", "row", "col"))
    plane = row_count * col_count
    experts = roles * plane
    row = lax.axis_index("row")
    expert = lax.axis_index(("role", "row", "col"))
    top = expert_ids.shape[2]

    def by_row(x, mask):
        return lax.ppermute(x, "row", [(i, i ^ mask) for i in range(row_count)])

    def by_plane(x, mask):
        return lax.ppermute(x, ("row", "col"), [(i, i ^ mask) for i in range(plane)])

    def by_role(x):
        return lax.ppermute(x, "role", [(i, i ^ 1) for i in range(roles)])

    order = jnp.bitwise_xor(row, jnp.arange(1, row_count, dtype=jnp.int32)).astype(jnp.int32)
    caches = (queries, cache_keys, prompt_value_cache, new_keys, fresh_token_values)
    foreign = attend(order, *caches)
    arrived = [by_row(foreign[m - 1], m) for m in range(1, row_count)]
    own = attend(row.astype(jnp.int32)[None], *caches)[0]
    *products, own_product = project(arrived + [own], out_weight, BF16)
    parts = [by_row(products[m - 1], m) for m in range(1, row_count)]

    gates = routing_gates[0]
    gates_high = lax.reduce_precision(gates, 8, 7)
    meta = jnp.concatenate([expert_ids[0].astype(F32), gates_high, gates - gates_high], axis=1)
    meta = jnp.pad(meta, ((0, 0), (0, -meta.shape[1] % LANES))).astype(BF16)
    mid_rows, token = norm_rows(own_product, parts, hidden, norm_gain, meta)

    half = col_count // 2
    members = [r * col_count + c for r in range(row_count) for c in range(half)]
    two_stage = row_count == 4 and half == 2
    mx, my, mz = col_count, 2 * col_count, 1

    def gather(x):
        if not two_stage:
            return {m: (by_plane(x, m) if m else x) for m in members}
        body = by_plane(x, mx ^ my ^ mz)
        bx, by, bz = by_plane(x, mx), by_plane(x, my), by_plane(x, mz)
        return {
            0: x,
            mx: bx,
            my: by,
            mz: bz,
            mx ^ my: by_plane(by, mx),
            my ^ mz: by_plane(bz, my),
            mz ^ mx: by_plane(bx, mz),
            mx ^ my ^ mz: body,
        }

    def scatter(y):
        if not two_stage:
            return add(*[by_plane(y[m], m) if m else y[m] for m in members])
        body = by_plane(y[mx ^ my ^ mz], mx ^ my ^ mz)
        via_x, via_y, via_z = by_plane(y[mx ^ my], mx), by_plane(y[my ^ mz], my), by_plane(y[mz ^ mx], mz)
        to_y = by_plane(add(y[my], via_x).astype(BF16), my)
        to_z = by_plane(add(y[mz], via_y).astype(BF16), mz)
        to_x = by_plane(add(y[mx], via_z).astype(BF16), mx)
        return add(y[0], body, to_x, to_y, to_z)

    numbers = jnp.stack([expert, jnp.bitwise_xor(expert, plane)]).astype(jnp.int32)
    weights = [[w, by_role(w)] for w in (expert_gate, expert_up, expert_down)]
    mirrored = by_plane(token, half)
    results = []
    for source in (token, mirrored):
        blocks = gather(source)
        partial = {}
        for first in range(0, len(members), 8):
            chunk = members[first : first + 8]
            outs = run_experts(numbers, [blocks[m] for m in chunk], *weights, top)
            partial.update(zip(chunk, outs))
        results.append(scatter(partial))
    returned = by_plane(results[1].astype(BF16), half)
    return (mid_rows + results[0] + returned.astype(F32)).astype(BF16)[None]


def solution(mesh):
    split = P(("role", "row", "col"), None, None)
    return jax.shard_map(
        per_device,
        mesh=mesh,
        in_specs=(split,) * 6 + (P("row", None), P()) + (split,) * 5,
        out_specs=split,
        check_vma=False,
    )
```
